32 devices in a mesh: sample: 2 (over x), row: 16 (over z, y, core).
Axes of the slice: x: 2, y: 2, z: 4, core: 2. Of those that a mesh axis runs over, the one named last changes fastest.
Arguments:
- sample_index: int32 [2], P('sample'), parts along dimension 0, may hold values from 0 to 32767
- lattice_vector: int32 [1024], replicated, may hold values from 1 to 32767
- mode_table: int32 [2, 1024], replicated, may hold values from -16 to 31, as said below
- connectivity: int32 [3, 32768], replicated, may hold values from 0 to 16639, as said below
- density: bfloat16 [64, 32768], P(None, 'row'), may hold values from -3.5 to 3.5
Outputs:
- potential: float32 [8192, 64], P(('sample', 'row')), parts along dimension 0
The draws below stay inside these ranges and needn't reach their ends.
There are 2 independent parts, one for each index of `sample`. The reference program is written for one: setup_inputs(seed, part) draws one part's arguments, and reference() takes and returns one part's arrays. A program takes and returns all parts, laid end to end along the dimension named above; an argument that names none is the same for every part. Nothing has to cross between parts.
Inputs may be any that keep to these rules, and one draw needn't show every extreme that they name: `mode_table`: the 1024 columns are distinct frequency pairs, the polar one from 0 to 31 and the azimuthal one from -16 to 15. `connectivity`: vertex i * 256 + j lies on latitude cycle i and azimuth j. The columns are the triangles of that grid, two per cell between neighbouring cycles (azimuth wrapping around), each once and oriented with outward normals, in random order.
All inputs are finite; a program needn't handle non-finite values.
Results may differ from the reference program's by a relative error of at most 0.0035.
Values may be sent and summed in bfloat16 or wider, within the bound.
A program may use at most 256 MiB of HBM per device.

```python
import math
import jax
import jax.numpy as jnp
from jax import lax

COLS = 64
MODES = 1024
NLAT = 32768
NPH = 256
SRC_DEV = 2048
BAND_DEV = 256
PANELS = 32768
BAND = 4096
NT = 65


def quad_layout(key):
    quad_total = (NT - 1) * NPH
    canonical = jnp.arange(2 * quad_total, dtype=jnp.int32)
    shuffled = jax.random.permutation(jax.random.fold_in(key, 11), canonical)
    quad_index = shuffled // 2
    return (quad_index // NPH, quad_index % NPH, shuffled % 2)


def draw_mode_table(key, part):
    chosen = jax.random.permutation(jax.random.fold_in(key, 1), jnp.arange(1024, dtype=jnp.int32))[:MODES]
    polar_freq = chosen // 32
    azim_freq = chosen % 32 - 16
    return jnp.stack([polar_freq, azim_freq]).astype(jnp.int32)


def draw_connectivity(key, part):
    cycle_index, column_index, upper_half = quad_layout(key)
    next_column = (column_index + 1) % NPH
    vertex_aa = cycle_index * NPH + column_index
    vertex_ba = (cycle_index + 1) * NPH + column_index
    vertex_ab = cycle_index * NPH + next_column
    vertex_bb = (cycle_index + 1) * NPH + next_column
    corner_one = jnp.where(upper_half == 0, vertex_aa, vertex_ba)
    corner_two = jnp.where(upper_half == 0, vertex_ba, vertex_bb)
    return jnp.stack([corner_one, corner_two, vertex_ab]).astype(jnp.int32)


def draw_density(key, part):
    cycle_index, column_index, upper_half = quad_layout(key)
    polar_mid = math.pi * (cycle_index.astype(jnp.float32) + 1.5) / (NT + 1)
    azim_mid = 2.0 * math.pi * (column_index.astype(jnp.float32) + 0.5) / NPH
    coef_one = jax.random.uniform(jax.random.fold_in(key, 31), (COLS, 1), jnp.float32, -0.8, 0.8)
    coef_two = jax.random.uniform(jax.random.fold_in(key, 32), (COLS, 1), jnp.float32, -0.8, 0.8)
    phase = jax.random.uniform(jax.random.fold_in(key, 33), (COLS, 1), jnp.float32, -math.pi, math.pi)
    sector_count = 2 ** jax.random.randint(jax.random.fold_in(key, 34), (COLS, 1), 1, 4)
    sector_offset = jax.random.randint(jax.random.fold_in(key, 35), (COLS, 1), 0, NPH)
    sector_index = (column_index[None, :] + sector_offset) % NPH * sector_count // NPH
    sector_sign = (1 - 2 * (sector_index % 2)).astype(jnp.float32)
    smooth = 0.6 + coef_one * jnp.cos(polar_mid)[None, :] + coef_two * jnp.sin(polar_mid)[None, :] * jnp.cos(azim_mid[None, :] - phase)
    level_key = jax.random.fold_in(key, 36)
    rough_key = jax.random.fold_in(key, 37)
    levels = jax.random.uniform(level_key, (COLS, 1), jnp.float32, 0.6, 1.2)
    rough = 0.25 * jnp.clip(jax.random.normal(rough_key, (COLS, PANELS), jnp.float32), -3.0, 3.0)
    return (levels * smooth * sector_sign + rough).astype(jnp.bfloat16)


def with_ends(values, own_key, smallest, high):
    longest = values.shape.index(max(values.shape))
    spots = []
    for shift in (0, 1):
        where = [jax.random.randint(jax.random.fold_in(own_key, axis), (), 0, length) for axis, length in enumerate(values.shape)]
        where[longest] = (where[longest] + shift) % values.shape[longest]
        spots.append(tuple(where))
    return values.at[spots[0]].set(smallest).at[spots[1]].set(high)


def setup_inputs(seed: int = 0, part: int = 0) -> dict:
    key_of = jax.random.split(jax.random.key(seed), 6)
    part_keys = jax.random.split(jax.random.fold_in(key_of[5], part), 6)
    return {
        "sample_index": jax.random.randint(part_keys[0], (1,), 0, NLAT).astype(jnp.int32),
        "lattice_vector": with_ends(jax.random.randint(key_of[1], (MODES,), 1, NLAT), jax.random.fold_in(key_of[1], 1), 1, NLAT - 1).astype(jnp.int32),
        "mode_table": draw_mode_table(jax.random.fold_in(key_of[5], 71), part),
        "connectivity": draw_connectivity(jax.random.fold_in(key_of[5], 71), part),
        "density": draw_density(jax.random.fold_in(key_of[5], 71), part),
    }


def vertex_grid(sample_index, lattice_vector, mode_table, cycle_count):
    lattice_steps = sample_index[0] * lattice_vector % NLAT
    shifts = lattice_steps.astype(jnp.float32) / NLAT - 0.5
    polar_freq = mode_table[0].astype(jnp.float32)
    azim_freq = mode_table[1].astype(jnp.float32)
    mode_coef = 0.8 * shifts / (1.0 + polar_freq + jnp.abs(azim_freq)) ** 2
    polar_angle = math.pi * (jnp.arange(cycle_count, dtype=jnp.float32) + 1.0) / (cycle_count + 1)
    azimuth = 2.0 * math.pi * jnp.arange(NPH, dtype=jnp.float32) / NPH
    polar_phase = polar_angle[:, None] * polar_freq[None, :]
    azim_phase = azim_freq[:, None] * azimuth[None, :]
    cos_part = jnp.dot(jnp.cos(polar_phase) * mode_coef[None, :], jnp.cos(azim_phase), precision=lax.Precision.HIGHEST)
    sin_part = jnp.dot(jnp.sin(polar_phase) * mode_coef[None, :], jnp.sin(azim_phase), precision=lax.Precision.HIGHEST)
    radius = jnp.exp(cos_part - sin_part)
    cycle_sin = jnp.sin(polar_angle)[:, None]
    coord_x = radius * cycle_sin * jnp.cos(azimuth)[None, :]
    coord_y = radius * cycle_sin * jnp.sin(azimuth)[None, :]
    coord_z = radius * jnp.cos(polar_angle)[:, None]
    return jnp.stack([coord_x, coord_y, coord_z]).reshape(3, cycle_count * NPH)

def panel_geometry(vertices, corners):
    corner_one = vertices[:, corners[0]]
    corner_two = vertices[:, corners[1]]
    corner_three = vertices[:, corners[2]]
    centers = (corner_one + corner_two + corner_three) / 3.0
    edge_one = corner_two - corner_one
    edge_two = corner_three - corner_one
    area_vectors = 0.5 * jnp.stack([edge_one[1] * edge_two[2] - edge_one[2] * edge_two[1], edge_one[2] * edge_two[0] - edge_one[0] * edge_two[2], edge_one[0] * edge_two[1] - edge_one[1] * edge_two[0]])
    return (centers, area_vectors)

def kernel_tile(target_centers, target_ids, source_centers, source_areas, source_ids):
    delta_x = target_centers[0][:, None] - source_centers[0][None, :]
    delta_y = target_centers[1][:, None] - source_centers[1][None, :]
    delta_z = target_centers[2][:, None] - source_centers[2][None, :]
    dist_sq = delta_x * delta_x + delta_y * delta_y + delta_z * delta_z
    self_pair = target_ids[:, None] == source_ids[None, :]
    safe_dist = jnp.where(self_pair, 1.0, dist_sq)
    numerator = delta_x * source_areas[0][None, :] + delta_y * source_areas[1][None, :] + delta_z * source_areas[2][None, :]
    kernel_value = numerator / (4.0 * math.pi * safe_dist * jnp.sqrt(safe_dist))
    return jnp.where(self_pair, 0.0, kernel_value).astype(jnp.bfloat16)

def reference(sample_index, lattice_vector, mode_table, connectivity, density):
    vertices = vertex_grid(sample_index, lattice_vector, mode_table, NT)
    centers, area_vectors = panel_geometry(vertices, connectivity)
    source_ids = jnp.arange(PANELS, dtype=jnp.int32)
    band_rows = jnp.arange(BAND, dtype=jnp.int32)
    band_panel = band_rows // BAND_DEV * SRC_DEV + band_rows % BAND_DEV
    block = math.gcd(BAND, 256)

    def one_block(turn):
        first_row = turn * block
        target_ids = lax.dynamic_slice_in_dim(band_panel, first_row, block, 0)
        target_centers = centers[:, target_ids]
        tile = kernel_tile(target_centers, target_ids, centers, area_vectors, source_ids)
        return lax.dot_general(tile, density, (((1,), (1,)), ((), ())), preferred_element_type=jnp.float32)
    sums = lax.map(one_block, jnp.arange(BAND // block, dtype=jnp.int32)).reshape(BAND, COLS)
    local_term = 0.5 * density[:, band_panel].astype(jnp.float32).T
    return local_term + sums
```

```python
import functools
import math

import jax
import jax.numpy as jnp
import numpy as np
from jax import lax
from jax.experimental import pallas as pl
from jax.experimental.pallas import tpu as pltpu
from jax.sharding import PartitionSpec as P

NLAT = 32768
NPH = 256
BAND_DEV = 256
POLAR = 32
AZIM = 32
AZIM_LOW = -16
KDIM = 32
CHUNK = 256
SRC_TILE = 256

F32 = jnp.float32
BF16 = jnp.bfloat16


def round_up(value, step):
    return -(-value // step) * step


def split3(value):
    high = value.astype(BF16)
    rest = value - high.astype(F32)
    mid = rest.astype(BF16)
    low = (rest - mid.astype(F32)).astype(BF16)
    return high, mid, low


def split3_np(value):
    import ml_dtypes

    value = value.astype(np.float32)
    high = value.astype(ml_dtypes.bfloat16)
    rest = value - high.astype(np.float32)
    mid = rest.astype(ml_dtypes.bfloat16)
    low = (rest - mid.astype(np.float32)).astype(ml_dtypes.bfloat16)
    return [high, mid, low]


def tables(cycle_count, padded):
    angle = np.pi * (np.arange(cycle_count) + 1.0) / (cycle_count + 1)
    azimuth = 2.0 * np.pi * np.arange(NPH) / NPH
    polar = np.arange(POLAR)
    azim = np.arange(AZIM) + AZIM_LOW
    pol = np.zeros((padded, 2 * POLAR), np.float32)
    pol[:cycle_count, :POLAR] = np.cos(angle[:, None] * polar[None])
    pol[:cycle_count, POLAR:] = np.sin(angle[:, None] * polar[None])
    azi = np.concatenate(
        [np.cos(azim[:, None] * azimuth[None]), -np.sin(azim[:, None] * azimuth[None])]
    ).astype(np.float32)
    after = np.roll(azimuth, -1)
    rows = []
    for field in (np.cos(azimuth), np.sin(azimuth), np.cos(after), np.sin(after)):
        rows += split3_np(field)
    azim_rows = np.zeros((16, NPH), rows[0].dtype)
    azim_rows[:12] = np.stack(rows)
    rows = []
    full = np.zeros(padded + 1)
    for func in (np.sin, np.cos):
        full[:cycle_count] = func(angle)
        rows += split3_np(full[:-1])
    for func in (np.sin, np.cos):
        full[:cycle_count] = func(angle)
        rows += split3_np(full[1:])
    polar_rows = np.zeros((16, padded), rows[0].dtype)
    polar_rows[:12] = np.stack(rows)
    return pol, azi, azim_rows, polar_rows


def dot_hi(left, right):
    return jnp.dot(left, right, precision=lax.Precision.HIGHEST, preferred_element_type=F32)


def geometry_kernel(
    padded, src_dev, row_total,
    sample_ref, lattice_ref, mode_ref, conn_ref, pol_ref, azi_ref, azim_rows_ref, polar_rows_ref,
    target_k_ref, target_c_ref, source_k_ref, source_b_ref,
    table_ref, rows_ref,
):
    steps = (sample_ref[0] * lattice_ref[...]) & (NLAT - 1)
    shifts = steps.astype(F32) / NLAT - 0.5
    polar = mode_ref[0:1, :]
    azim = mode_ref[1:2, :]
    scale = 1.0 + polar.astype(F32) + jnp.abs(azim.astype(F32))
    coef = 0.8 * shifts / (scale * scale)
    modes = coef.shape[1]
    at_polar = lax.broadcasted_iota(jnp.int32, (POLAR, modes), 0) == polar
    at_azim = lax.broadcasted_iota(jnp.int32, (AZIM, modes), 0) + AZIM_LOW == azim
    azim_hot = jnp.where(at_azim, 1.0, 0.0).astype(BF16)
    grid = jnp.zeros((POLAR, AZIM), F32)
    for part in split3(jnp.where(at_polar, coef, 0.0)):
        grid += lax.dot_general(part, azim_hot, (((1,), (1,)), ((), ())), preferred_element_type=F32)
    cos_half = dot_hi(grid, azi_ref[0:AZIM, :])
    sin_half = dot_hi(grid, azi_ref[AZIM:2 * AZIM, :])
    log_radius = dot_hi(pol_ref[:, 0:POLAR], cos_half) + dot_hi(pol_ref[:, POLAR:2 * POLAR], sin_half)
    radius = jnp.exp(log_radius)
    after = pltpu.roll(radius, NPH - 1, 1)
    for index, part in enumerate(split3(radius) + split3(after)):
        table_ref[index * padded:(index + 1) * padded, :] = part
    table_ref[6 * padded:6 * padded + 16, :] = azim_rows_ref[...]
    rows_ref[...] = jnp.zeros_like(rows_ref)

    def corners_of(corner):
        azim_all = corner & (NPH - 1)
        cycle_all = corner // NPH
        azim_k = [azim_all[k:k + 1, :] for k in range(3)]
        cycle_k = [cycle_all[k:k + 1, :] for k in range(3)]
        cycle0 = jnp.minimum(jnp.minimum(cycle_k[0], cycle_k[1]), cycle_k[2])
        low = jnp.minimum(jnp.minimum(azim_k[0], azim_k[1]), azim_k[2])
        high = jnp.maximum(jnp.maximum(azim_k[0], azim_k[1]), azim_k[2])
        azim0 = jnp.where(high - low > 1, high, low)
        hot = jnp.where(
            lax.broadcasted_iota(jnp.int32, (NPH, CHUNK), 0) == azim0, 1.0, 0.0
        ).astype(BF16)
        picked = jnp.dot(table_ref[...], hot, preferred_element_type=F32)
        near = picked[0:padded] + picked[padded:2 * padded] + picked[2 * padded:3 * padded]
        far = picked[3 * padded:4 * padded] + picked[4 * padded:5 * padded] + picked[5 * padded:6 * padded]
        tail = picked[6 * padded:6 * padded + 16]
        cycles = lax.broadcasted_iota(jnp.int32, (padded, CHUNK), 0)
        here = cycles == cycle0
        below = cycles == cycle0 + 1

        def take(mask, field):
            return jnp.sum(jnp.where(mask, field, 0.0), axis=0, keepdims=True)

        radius_of = ((take(here, near), take(here, far)), (take(below, near), take(below, far)))
        cycle_hot = jnp.where(here, 1.0, 0.0).astype(BF16)
        turn = jnp.dot(polar_rows_ref[...], cycle_hot, preferred_element_type=F32)

        def join(rows, start):
            return rows[start:start + 1] + rows[start + 1:start + 2] + rows[start + 2:start + 3]

        sin_t = (join(turn, 0), join(turn, 6))
        cos_t = (join(turn, 3), join(turn, 9))
        cos_f = (join(tail, 0), join(tail, 6))
        sin_f = (join(tail, 3), join(tail, 9))
        points = []
        for k in range(3):
            down = cycle_k[k] != cycle0
            side = azim_k[k] != azim0
            radius_k = jnp.where(
                down,
                jnp.where(side, radius_of[1][1], radius_of[1][0]),
                jnp.where(side, radius_of[0][1], radius_of[0][0]),
            )
            ring = radius_k * jnp.where(down, sin_t[1], sin_t[0])
            points.append((
                ring * jnp.where(side, cos_f[1], cos_f[0]),
                ring * jnp.where(side, sin_f[1], sin_f[0]),
                radius_k * jnp.where(down, cos_t[1], cos_t[0]),
            ))
        return points

    def center_of(points):
        return [(points[0][axis] + points[1][axis] + points[2][axis]) / 3.0 for axis in range(3)]

    def target_chunk(turn, carry):
        first = pl.multiple_of(turn * src_dev, src_dev)
        center = center_of(corners_of(conn_ref[:, pl.ds(first, CHUNK)]))
        place = pl.ds(pl.multiple_of(turn * CHUNK, CHUNK), CHUNK)
        for axis in range(3):
            target_c_ref[axis:axis + 1, place] = center[axis]
            high, mid, low = [part.astype(F32) for part in split3(center[axis])]
            for index, part in enumerate((high, high, high, mid, mid, low)):
                rows_ref[6 * axis + index:6 * axis + index + 1, :] = part
        rows_ref[18:21, :] = jnp.ones((3, CHUNK), F32)
        target_k_ref[:, place] = rows_ref[0:KDIM, :].astype(BF16)
        return carry

    def source_chunk(turn, carry):
        first = pl.multiple_of(lax.axis_index("row") * src_dev + turn * CHUNK, CHUNK)
        points = corners_of(conn_ref[:, pl.ds(first, CHUNK)])
        center = center_of(points)
        one = [points[1][axis] - points[0][axis] for axis in range(3)]
        two = [points[2][axis] - points[0][axis] for axis in range(3)]
        factor = 0.5 / (4.0 * math.pi)
        area = [
            factor * (one[1] * two[2] - one[2] * two[1]),
            factor * (one[2] * two[0] - one[0] * two[2]),
            factor * (one[0] * two[1] - one[1] * two[0]),
        ]
        for axis in range(3):
            high, mid, low = [part.astype(F32) for part in split3(area[axis])]
            for index, part in enumerate((high, mid, low, high, mid, high)):
                rows_ref[6 * axis + index:6 * axis + index + 1, :] = part
        base = -(center[0] * area[0] + center[1] * area[1] + center[2] * area[2])
        for index, part in enumerate(split3(base)):
            rows_ref[18 + index:19 + index, :] = part.astype(F32)
        for axis in range(3):
            rows_ref[KDIM + axis:KDIM + axis + 1, :] = center[axis]
        turned = rows_ref[...].T
        place = pl.ds(pl.multiple_of(turn * CHUNK, CHUNK), CHUNK)
        source_k_ref[place, :] = turned[:, 0:KDIM].astype(BF16)
        for axis in range(3):
            source_b_ref[axis, place, :] = jnp.broadcast_to(
                turned[:, KDIM + axis:KDIM + axis + 1], (CHUNK, 128)
            )
        return carry

    lax.fori_loop(0, row_total, target_chunk, 0)
    lax.fori_loop(0, src_dev // CHUNK, source_chunk, 0)


def pair_kernel(
    src_dev, row_total,
    target_k_ref, target_c_ref, source_k_ref, source_b_ref, density_ref,
    out_ref, send_buf, recv_buf, send_sem, recv_sem,
):
    me = lax.axis_index("row")
    peers = row_total - 1

    barrier = pltpu.get_barrier_semaphore()

    def greet(turn, carry):
        other = lax.rem(me + 1 + turn, row_total)
        pl.semaphore_signal(
            barrier, inc=1, device_id={"row": other}, device_id_type=pl.DeviceIdType.MESH
        )
        return carry

    lax.fori_loop(0, peers, greet, 0)

    def block(owner, own):
        place = pl.ds(pl.multiple_of(owner * BAND_DEV, BAND_DEV), BAND_DEV)
        target_k = target_k_ref[:, place]
        target = [target_c_ref[axis:axis + 1, place] for axis in range(3)]
        total = jnp.zeros((density_ref.shape[0], BAND_DEV), F32)
        for first in range(0, src_dev, SRC_TILE):
            part = slice(first, first + SRC_TILE)
            top = jnp.dot(source_k_ref[part, :], target_k, preferred_element_type=F32)
            dist = None
            for axis in range(3):
                wide = source_b_ref[axis, part, :]
                diff = target[axis] - jnp.concatenate([wide] * (BAND_DEV // 128), axis=1)
                dist = diff * diff if dist is None else dist + diff * diff
            if own and first < BAND_DEV:
                same = (
                    lax.broadcasted_iota(jnp.int32, dist.shape, 0) + first
                    == lax.broadcasted_iota(jnp.int32, dist.shape, 1)
                )
                inverse = lax.rsqrt(jnp.where(same, 1.0, dist))
                tile = jnp.where(same, 0.0, top * inverse * (inverse * inverse))
            else:
                inverse = lax.rsqrt(dist)
                tile = top * inverse * (inverse * inverse)
            total += jnp.dot(density_ref[:, part], tile.astype(BF16), preferred_element_type=F32)
        return total

    def copy(turn):
        return pltpu.make_async_remote_copy(
            src_ref=send_buf.at[turn],
            dst_ref=recv_buf.at[turn],
            send_sem=send_sem.at[turn],
            recv_sem=recv_sem.at[turn],
            device_id={"row": lax.rem(me + 1 + turn, row_total)},
            device_id_type=pl.DeviceIdType.MESH,
        )

    send_buf[0] = block(lax.rem(me + 1, row_total), False).astype(BF16)
    pl.semaphore_wait(barrier, peers)
    copy(0).start()

    def step(turn, carry):
        send_buf[turn] = block(lax.rem(me + 1 + turn, row_total), False).astype(BF16)
        copy(turn).start()
        return carry

    lax.fori_loop(1, peers, step, 0)
    out_ref[...] = block(me, True) + 0.5 * density_ref[:, 0:BAND_DEV].astype(F32)

    def collect(turn, carry):
        copy(turn).wait_recv()
        out_ref[...] += recv_buf[turn].astype(F32)
        return carry

    lax.fori_loop(0, peers, collect, 0)

    def finish(turn, carry):
        copy(turn).wait_send()
        return carry

    lax.fori_loop(0, peers, finish, 0)


def per_device(sample_index, lattice_vector, mode_table, connectivity, density):
    columns, src_dev = density.shape
    row_total = lax.axis_size("row")
    panel_total = src_dev * row_total
    cycle_count = panel_total // (2 * NPH) + 1
    padded = round_up(cycle_count, 16)
    band = BAND_DEV * row_total
    pol, azi, azim_rows, polar_rows = [jnp.asarray(t) for t in tables(cycle_count, padded)]
    vmem = pl.BlockSpec(memory_space=pltpu.VMEM)
    smem = pl.BlockSpec(memory_space=pltpu.SMEM)
    target_k, target_c, source_k, source_b = pl.pallas_call(
        functools.partial(geometry_kernel, padded, src_dev, row_total),
        out_shape=[
            jax.ShapeDtypeStruct((KDIM, band), BF16),
            jax.ShapeDtypeStruct((3, band), F32),
            jax.ShapeDtypeStruct((src_dev, KDIM), BF16),
            jax.ShapeDtypeStruct((3, src_dev, 128), F32),
        ],
        in_specs=[smem] + [vmem] * 7,
        out_specs=[vmem] * 4,
        scratch_shapes=[
            pltpu.VMEM((6 * padded + 16, NPH), BF16),
            pltpu.VMEM((KDIM + 8, CHUNK), F32),
        ],
        compiler_params=pltpu.CompilerParams(vmem_limit_bytes=40 << 20),
        name="geometry",
    )(
        sample_index, lattice_vector.reshape(1, -1), mode_table, connectivity,
        pol, azi, azim_rows, polar_rows,
    )
    sums = pl.pallas_call(
        functools.partial(pair_kernel, src_dev, row_total),
        out_shape=jax.ShapeDtypeStruct((columns, BAND_DEV), F32),
        in_specs=[vmem] * 5,
        out_specs=vmem,
        scratch_shapes=[
            pltpu.VMEM((row_total - 1, columns, BAND_DEV), BF16),
            pltpu.VMEM((row_total - 1, columns, BAND_DEV), BF16),
            pltpu.SemaphoreType.DMA((row_total - 1,)),
            pltpu.SemaphoreType.DMA((row_total - 1,)),
        ],
        compiler_params=pltpu.CompilerParams(
            collective_id=0, has_side_effects=True, vmem_limit_bytes=40 << 20
        ),
        name="pairs",
    )(target_k, target_c, source_k, source_b, density)
    return sums.T


def solution(mesh):
    placed = (P("sample"), P(), P(), P(), P(None, "row"))
    return jax.shard_map(
        per_device,
        mesh=mesh,
        in_specs=placed,
        out_specs=P(("sample", "row"), None),
        check_vma=False,
    )
```

```python
import functools
import math

import jax
import jax.numpy as jnp
import numpy as np
from jax import lax
from jax.experimental import pallas as pl
from jax.experimental.pallas import tpu as pltpu
from jax.sharding import PartitionSpec as P

NLAT = 32768
NPH = 256
BAND_DEV = 256
POLAR = 32
AZIM = 32
AZIM_LOW = -16
KDIM = 32
CHUNK = 256
SRC_TILE = 512

F32 = jnp.float32
BF16 = jnp.bfloat16


def round_up(value, step):
    return -(-value // step) * step


def split3(value):
    high = value.astype(BF16)
    rest = value - high.astype(F32)
    mid = rest.astype(BF16)
    low = (rest - mid.astype(F32)).astype(BF16)
    return high, mid, low


def split3_np(value):
    import ml_dtypes

    value = value.astype(np.float32)
    high = value.astype(ml_dtypes.bfloat16)
    rest = value - high.astype(np.float32)
    mid = rest.astype(ml_dtypes.bfloat16)
    low = (rest - mid.astype(np.float32)).astype(ml_dtypes.bfloat16)
    return [high, mid, low]


def tables(cycle_count, padded):
    angle = np.pi * (np.arange(cycle_count) + 1.0) / (cycle_count + 1)
    azimuth = 2.0 * np.pi * np.arange(NPH) / NPH
    polar = np.arange(POLAR)
    azim = np.arange(AZIM) + AZIM_LOW
    pol = np.zeros((padded, 2 * POLAR), np.float32)
    pol[:cycle_count, :POLAR] = np.cos(angle[:, None] * polar[None])
    pol[:cycle_count, POLAR:] = np.sin(angle[:, None] * polar[None])
    azi = np.concatenate(
        [np.cos(azim[:, None] * azimuth[None]), -np.sin(azim[:, None] * azimuth[None])]
    ).astype(np.float32)
    after = np.roll(azimuth, -1)
    rows = []
    for field in (np.cos(azimuth), np.sin(azimuth), np.cos(after), np.sin(after)):
        rows += split3_np(field)
    azim_rows = np.zeros((16, NPH), rows[0].dtype)
    azim_rows[:12] = np.stack(rows)
    rows = []
    full = np.zeros(padded + 1)
    for func in (np.sin, np.cos):
        full[:cycle_count] = func(angle)
        rows += split3_np(full[:-1])
    for func in (np.sin, np.cos):
        full[:cycle_count] = func(angle)
        rows += split3_np(full[1:])
    polar_rows = np.zeros((16, padded), rows[0].dtype)
    polar_rows[:12] = np.stack(rows)
    return pol, azi, azim_rows, polar_rows


def dot_hi(left, right):
    return jnp.dot(left, right, precision=lax.Precision.HIGHEST, preferred_element_type=F32)


def geometry(
    padded, src_dev, row_total, wait_conn,
    sample_ref, lattice_ref, mode_ref, conn_ref, pol_ref, azi_ref, azim_rows_ref, polar_rows_ref,
    target_k_ref, target_c_ref, source_k_ref, source_b_ref,
    table_ref, rows_ref,
):
    steps = (sample_ref[0] * lattice_ref[...]) & (NLAT - 1)
    shifts = steps.astype(F32) / NLAT - 0.5
    polar = mode_ref[0:1, :]
    azim = mode_ref[1:2, :]
    scale = 1.0 + polar.astype(F32) + jnp.abs(azim.astype(F32))
    coef = 0.8 * shifts / (scale * scale)
    modes = coef.shape[1]
    at_polar = lax.broadcasted_iota(jnp.int32, (POLAR, modes), 0) == polar
    at_azim = lax.broadcasted_iota(jnp.int32, (AZIM, modes), 0) + AZIM_LOW == azim
    azim_hot = jnp.where(at_azim, 1.0, 0.0).astype(BF16)
    grid = jnp.zeros((POLAR, AZIM), F32)
    for part in split3(jnp.where(at_polar, coef, 0.0)):
        grid += lax.dot_general(part, azim_hot, (((1,), (1,)), ((), ())), preferred_element_type=F32)
    cos_half = dot_hi(grid, azi_ref[0:AZIM, :])
    sin_half = dot_hi(grid, azi_ref[AZIM:2 * AZIM, :])
    log_radius = dot_hi(pol_ref[:, 0:POLAR], cos_half) + dot_hi(pol_ref[:, POLAR:2 * POLAR], sin_half)
    radius = jnp.exp(log_radius)
    after = pltpu.roll(radius, NPH - 1, 1)
    for index, part in enumerate(split3(radius) + split3(after)):
        table_ref[index * padded:(index + 1) * padded, :] = part
    table_ref[6 * padded:6 * padded + 16, :] = azim_rows_ref[...]
    rows_ref[...] = jnp.zeros_like(rows_ref)
    wait_conn()

    def corners_of(corner):
        azim_all = corner & (NPH - 1)
        cycle_all = corner // NPH
        azim_k = [azim_all[k:k + 1, :] for k in range(3)]
        cycle_k = [cycle_all[k:k + 1, :] for k in range(3)]
        cycle0 = jnp.minimum(jnp.minimum(cycle_k[0], cycle_k[1]), cycle_k[2])
        low = jnp.minimum(jnp.minimum(azim_k[0], azim_k[1]), azim_k[2])
        high = jnp.maximum(jnp.maximum(azim_k[0], azim_k[1]), azim_k[2])
        azim0 = jnp.where(high - low > 1, high, low)
        hot = jnp.where(
            lax.broadcasted_iota(jnp.int32, (NPH, CHUNK), 0) == azim0, 1.0, 0.0
        ).astype(BF16)
        picked = jnp.dot(table_ref[...], hot, preferred_element_type=F32)
        near = picked[0:padded] + picked[padded:2 * padded] + picked[2 * padded:3 * padded]
        far = picked[3 * padded:4 * padded] + picked[4 * padded:5 * padded] + picked[5 * padded:6 * padded]
        tail = picked[6 * padded:6 * padded + 16]
        cycles = lax.broadcasted_iota(jnp.int32, (padded, CHUNK), 0)
        here = cycles == cycle0
        below = cycles == cycle0 + 1

        def take(mask, field):
            return jnp.sum(jnp.where(mask, field, 0.0), axis=0, keepdims=True)

        radius_of = ((take(here, near), take(here, far)), (take(below, near), take(below, far)))
        cycle_hot = jnp.where(here, 1.0, 0.0).astype(BF16)
        turn = jnp.dot(polar_rows_ref[...], cycle_hot, preferred_element_type=F32)

        def join(rows, start):
            return rows[start:start + 1] + rows[start + 1:start + 2] + rows[start + 2:start + 3]

        sin_t = (join(turn, 0), join(turn, 6))
        cos_t = (join(turn, 3), join(turn, 9))
        cos_f = (join(tail, 0), join(tail, 6))
        sin_f = (join(tail, 3), join(tail, 9))
        points = []
        for k in range(3):
            down = cycle_k[k] != cycle0
            side = azim_k[k] != azim0
            radius_k = jnp.where(
                down,
                jnp.where(side, radius_of[1][1], radius_of[1][0]),
                jnp.where(side, radius_of[0][1], radius_of[0][0]),
            )
            ring = radius_k * jnp.where(down, sin_t[1], sin_t[0])
            points.append((
                ring * jnp.where(side, cos_f[1], cos_f[0]),
                ring * jnp.where(side, sin_f[1], sin_f[0]),
                radius_k * jnp.where(down, cos_t[1], cos_t[0]),
            ))
        return points

    def center_of(points):
        return [(points[0][axis] + points[1][axis] + points[2][axis]) / 3.0 for axis in range(3)]

    def target_chunk(turn, carry):
        first = pl.multiple_of(turn * src_dev, src_dev)
        center = center_of(corners_of(conn_ref[:, pl.ds(first, CHUNK)]))
        place = pl.ds(pl.multiple_of(turn * CHUNK, CHUNK), CHUNK)
        for axis in range(3):
            target_c_ref[axis:axis + 1, place] = center[axis]
            high, mid, low = [part.astype(F32) for part in split3(center[axis])]
            for index, part in enumerate((high, high, high, mid, mid, low)):
                rows_ref[6 * axis + index:6 * axis + index + 1, :] = part
        rows_ref[18:21, :] = jnp.ones((3, CHUNK), F32)
        target_k_ref[:, place] = rows_ref[0:KDIM, :].astype(BF16)
        return carry

    def source_chunk(turn, carry):
        first = pl.multiple_of(lax.axis_index("row") * src_dev + turn * CHUNK, CHUNK)
        points = corners_of(conn_ref[:, pl.ds(first, CHUNK)])
        center = center_of(points)
        one = [points[1][axis] - points[0][axis] for axis in range(3)]
        two = [points[2][axis] - points[0][axis] for axis in range(3)]
        factor = 0.5 / (4.0 * math.pi)
        area = [
            factor * (one[1] * two[2] - one[2] * two[1]),
            factor * (one[2] * two[0] - one[0] * two[2]),
            factor * (one[0] * two[1] - one[1] * two[0]),
        ]
        for axis in range(3):
            high, mid, low = [part.astype(F32) for part in split3(area[axis])]
            for index, part in enumerate((high, mid, low, high, mid, high)):
                rows_ref[6 * axis + index:6 * axis + index + 1, :] = part
        base = -(center[0] * area[0] + center[1] * area[1] + center[2] * area[2])
        for index, part in enumerate(split3(base)):
            rows_ref[18 + index:19 + index, :] = part.astype(F32)
        for axis in range(3):
            rows_ref[KDIM + axis:KDIM + axis + 1, :] = center[axis]
        turned = rows_ref[...].T
        place = pl.ds(pl.multiple_of(turn * CHUNK, CHUNK), CHUNK)
        source_k_ref[place, :] = turned[:, 0:KDIM].astype(BF16)
        for axis in range(3):
            source_b_ref[axis, place, :] = jnp.broadcast_to(
                turned[:, KDIM + axis:KDIM + axis + 1], (CHUNK, 128)
            )
        return carry

    lax.fori_loop(0, row_total, target_chunk, 0, unroll=4)
    lax.fori_loop(0, src_dev // CHUNK, source_chunk, 0, unroll=4)


def kernel(
    padded, src_dev, row_total,
    sample_ref, conn_hbm, density_hbm, lattice_hbm, mode_hbm, pol_hbm, azi_hbm, azim_rows_hbm,
    polar_rows_hbm,
    out_ref,
    conn_ref, density_ref, lattice_ref, mode_ref, pol_ref, azi_ref, azim_rows_ref, polar_rows_ref,
    target_k_ref, target_c_ref, source_k_ref, source_b_ref, table_ref, rows_ref,
    send_buf, recv_buf, load_sem, send_sem, recv_sem,
):
    loads = [
        pltpu.make_async_copy(source, place, load_sem.at[index])
        for index, (source, place) in enumerate((
            (conn_hbm, conn_ref), (density_hbm, density_ref), (lattice_hbm, lattice_ref),
            (mode_hbm, mode_ref), (pol_hbm, pol_ref), (azi_hbm, azi_ref),
            (azim_rows_hbm, azim_rows_ref), (polar_rows_hbm, polar_rows_ref),
        ))
    ]
    for index in (3, 2, 5, 4, 6, 7, 0, 1):
        loads[index].start()
    me = lax.axis_index("row")
    peers = row_total - 1

    barrier = pltpu.get_barrier_semaphore()

    def greet(turn, carry):
        other = lax.rem(me + 1 + turn, row_total)
        pl.semaphore_signal(
            barrier, inc=1, device_id={"row": other}, device_id_type=pl.DeviceIdType.MESH
        )
        return carry

    lax.fori_loop(0, peers, greet, 0)
    for load in loads[2:]:
        load.wait()
    geometry(
        padded, src_dev, row_total, loads[0].wait,
        sample_ref, lattice_ref, mode_ref, conn_ref, pol_ref, azi_ref, azim_rows_ref,
        polar_rows_ref, target_k_ref, target_c_ref, source_k_ref, source_b_ref,
        table_ref, rows_ref,
    )
    loads[1].wait()

    def block(owner, own):
        place = pl.ds(pl.multiple_of(owner * BAND_DEV, BAND_DEV), BAND_DEV)
        target_k = target_k_ref[:, place]
        target = [target_c_ref[axis:axis + 1, place] for axis in range(3)]
        def numerator(first):
            return jnp.dot(
                source_k_ref[first:first + SRC_TILE, :], target_k, preferred_element_type=F32
            )

        def weigh(first, tile):
            return jnp.dot(
                density_ref[:, first:first + SRC_TILE], tile, preferred_element_type=F32
            )

        total = jnp.zeros((density_ref.shape[0], BAND_DEV), F32)
        top = numerator(0)
        before = None
        for first in range(0, src_dev, SRC_TILE):
            following = numerator(first + SRC_TILE) if first + SRC_TILE < src_dev else None
            part = slice(first, first + SRC_TILE)
            dist = None
            for axis in range(3):
                wide = source_b_ref[axis, part, :]
                diff = target[axis] - jnp.concatenate([wide] * (BAND_DEV // 128), axis=1)
                dist = diff * diff if dist is None else dist + diff * diff
            if own and first < BAND_DEV:
                same = (
                    lax.broadcasted_iota(jnp.int32, dist.shape, 0) + first
                    == lax.broadcasted_iota(jnp.int32, dist.shape, 1)
                )
                inverse = lax.rsqrt(jnp.where(same, 1.0, dist))
                tile = jnp.where(same, 0.0, top * inverse * (inverse * inverse))
            else:
                inverse = lax.rsqrt(dist)
                tile = top * inverse * (inverse * inverse)
            tile = tile.astype(BF16)
            if before is not None:
                total += weigh(first - SRC_TILE, before)
            before = tile
            top = following
        return total + weigh(src_dev - SRC_TILE, before)

    def copy(turn):
        return pltpu.make_async_remote_copy(
            src_ref=send_buf.at[turn],
            dst_ref=recv_buf.at[turn],
            send_sem=send_sem.at[turn],
            recv_sem=recv_sem.at[turn],
            device_id={"row": lax.rem(me + 1 + turn, row_total)},
            device_id_type=pl.DeviceIdType.MESH,
        )

    send_buf[0] = block(lax.rem(me + 1, row_total), False).astype(BF16)
    pl.semaphore_wait(barrier, peers)
    copy(0).start()

    def step(turn, carry):
        send_buf[turn] = block(lax.rem(me + 1 + turn, row_total), False).astype(BF16)
        copy(turn).start()
        return carry

    lax.fori_loop(1, peers, step, 0)
    out_ref[...] = block(me, True) + 0.5 * density_ref[:, 0:BAND_DEV].astype(F32)

    def collect(turn, carry):
        copy(turn).wait_recv()
        out_ref[...] += recv_buf[turn].astype(F32)
        return carry

    lax.fori_loop(0, peers, collect, 0)

    def finish(turn, carry):
        copy(turn).wait_send()
        return carry

    lax.fori_loop(0, peers, finish, 0)


def per_device(sample_index, lattice_vector, mode_table, connectivity, density):
    columns, src_dev = density.shape
    row_total = lax.axis_size("row")
    panel_total = src_dev * row_total
    cycle_count = panel_total // (2 * NPH) + 1
    padded = round_up(cycle_count, 16)
    band = BAND_DEV * row_total
    pol, azi, azim_rows, polar_rows = [jnp.asarray(t) for t in tables(cycle_count, padded)]
    vmem = pl.BlockSpec(memory_space=pltpu.VMEM)
    smem = pl.BlockSpec(memory_space=pltpu.SMEM)
    hbm = pl.BlockSpec(memory_space=pltpu.HBM)
    loaded = [
        connectivity, density, lattice_vector.reshape(1, -1), mode_table,
        pol, azi, azim_rows, polar_rows,
    ]
    sums = pl.pallas_call(
        functools.partial(kernel, padded, src_dev, row_total),
        out_shape=jax.ShapeDtypeStruct((columns, BAND_DEV), F32),
        in_specs=[smem] + [hbm] * len(loaded),
        out_specs=vmem,
        scratch_shapes=[pltpu.VMEM(array.shape, array.dtype) for array in loaded] + [
            pltpu.VMEM((KDIM, band), BF16),
            pltpu.VMEM((3, band), F32),
            pltpu.VMEM((src_dev, KDIM), BF16),
            pltpu.VMEM((3, src_dev, 128), F32),
            pltpu.VMEM((6 * padded + 16, NPH), BF16),
            pltpu.VMEM((KDIM + 8, CHUNK), F32),
            pltpu.VMEM((row_total - 1, columns, BAND_DEV), BF16),
            pltpu.VMEM((row_total - 1, columns, BAND_DEV), BF16),
            pltpu.SemaphoreType.DMA((len(loaded),)),
            pltpu.SemaphoreType.DMA((row_total - 1,)),
            pltpu.SemaphoreType.DMA((row_total - 1,)),
        ],
        compiler_params=pltpu.CompilerParams(
            collective_id=0, has_side_effects=True, vmem_limit_bytes=40 << 20
        ),
        name="potential",
    )(sample_index, *loaded)
    return sums.T


def solution(mesh):
    placed = (P("sample"), P(), P(), P(), P(None, "row"))
    return jax.shard_map(
        per_device,
        mesh=mesh,
        in_specs=placed,
        out_specs=P(("sample", "row"), None),
        check_vma=False,
    )
```

```python
import functools
import math

import jax
import jax.numpy as jnp
import numpy as np
from jax import lax
from jax.experimental import pallas as pl
from jax.experimental.pallas import tpu as pltpu
from jax.sharding import PartitionSpec as P

NLAT = 32768
NPH = 256
BAND_DEV = 256
POLAR = 32
AZIM = 32
AZIM_LOW = -16
KDIM = 32
CHUNK = 256
SRC_TILE = 512

F32 = jnp.float32
BF16 = jnp.bfloat16


def round_up(value, step):
    return -(-value // step) * step


def split3(value):
    high = value.astype(BF16)
    rest = value - high.astype(F32)
    mid = rest.astype(BF16)
    low = (rest - mid.astype(F32)).astype(BF16)
    return high, mid, low


def split3_np(value):
    import ml_dtypes

    value = value.astype(np.float32)
    high = value.astype(ml_dtypes.bfloat16)
    rest = value - high.astype(np.float32)
    mid = rest.astype(ml_dtypes.bfloat16)
    low = (rest - mid.astype(np.float32)).astype(ml_dtypes.bfloat16)
    return [high, mid, low]


def tables(cycle_count, padded):
    angle = np.pi * (np.arange(cycle_count) + 1.0) / (cycle_count + 1)
    azimuth = 2.0 * np.pi * np.arange(NPH) / NPH
    polar = np.arange(POLAR)
    azim = np.arange(AZIM) + AZIM_LOW
    pol = np.zeros((padded, 2 * POLAR), np.float32)
    pol[:cycle_count, :POLAR] = np.cos(angle[:, None] * polar[None])
    pol[:cycle_count, POLAR:] = np.sin(angle[:, None] * polar[None])
    azi = np.concatenate(
        [np.cos(azim[:, None] * azimuth[None]), -np.sin(azim[:, None] * azimuth[None])]
    ).astype(np.float32)
    after = np.roll(azimuth, -1)
    rows = []
    for field in (np.cos(azimuth), np.sin(azimuth), np.cos(after), np.sin(after)):
        rows += split3_np(field)
    azim_rows = np.zeros((16, NPH), rows[0].dtype)
    azim_rows[:12] = np.stack(rows)
    rows = []
    full = np.zeros(padded + 1)
    for func in (np.sin, np.cos):
        full[:cycle_count] = func(angle)
        rows += split3_np(full[:-1])
    for func in (np.sin, np.cos):
        full[:cycle_count] = func(angle)
        rows += split3_np(full[1:])
    polar_rows = np.zeros((16, padded), rows[0].dtype)
    polar_rows[:12] = np.stack(rows)
    return pol, azi, azim_rows, polar_rows


def dot_hi(left, right):
    return jnp.dot(left, right, precision=lax.Precision.HIGHEST, preferred_element_type=F32)


def geometry(
    padded, src_dev, row_total, wait_conn,
    sample_ref, lattice_ref, mode_ref, conn_ref, pol_ref, azi_ref, azim_rows_ref, polar_rows_ref,
    target_k_ref, target_c_ref, source_k_ref, source_b_ref,
    table_ref, rows_ref,
):
    me = lax.axis_index("row")
    side_of_pair = lax.rem(me, 2)
    steps = (sample_ref[0] * lattice_ref[...]) & (NLAT - 1)
    shifts = steps.astype(F32) / NLAT - 0.5
    polar = mode_ref[0:1, :]
    azim = mode_ref[1:2, :]
    scale = 1.0 + polar.astype(F32) + jnp.abs(azim.astype(F32))
    coef = 0.8 * shifts / (scale * scale)
    modes = coef.shape[1]
    at_polar = lax.broadcasted_iota(jnp.int32, (POLAR, modes), 0) == polar
    at_azim = lax.broadcasted_iota(jnp.int32, (AZIM, modes), 0) + AZIM_LOW == azim
    azim_hot = jnp.where(at_azim, 1.0, 0.0).astype(BF16)
    grid = jnp.zeros((POLAR, AZIM), F32)
    for part in split3(jnp.where(at_polar, coef, 0.0)):
        grid += lax.dot_general(part, azim_hot, (((1,), (1,)), ((), ())), preferred_element_type=F32)
    cos_half = dot_hi(grid, azi_ref[0:AZIM, :])
    sin_half = dot_hi(grid, azi_ref[AZIM:2 * AZIM, :])
    log_radius = dot_hi(pol_ref[:, 0:POLAR], cos_half) + dot_hi(pol_ref[:, POLAR:2 * POLAR], sin_half)
    radius = jnp.exp(log_radius)
    after = pltpu.roll(radius, NPH - 1, 1)
    for index, part in enumerate(split3(radius) + split3(after)):
        table_ref[index * padded:(index + 1) * padded, :] = part
    table_ref[6 * padded:6 * padded + 16, :] = azim_rows_ref[...]
    rows_ref[...] = jnp.zeros_like(rows_ref)
    wait_conn()

    def corners_of(corner):
        azim_all = corner & (NPH - 1)
        cycle_all = corner // NPH
        azim_k = [azim_all[k:k + 1, :] for k in range(3)]
        cycle_k = [cycle_all[k:k + 1, :] for k in range(3)]
        cycle0 = jnp.minimum(jnp.minimum(cycle_k[0], cycle_k[1]), cycle_k[2])
        low = jnp.minimum(jnp.minimum(azim_k[0], azim_k[1]), azim_k[2])
        high = jnp.maximum(jnp.maximum(azim_k[0], azim_k[1]), azim_k[2])
        azim0 = jnp.where(high - low > 1, high, low)
        hot = jnp.where(
            lax.broadcasted_iota(jnp.int32, (NPH, CHUNK), 0) == azim0, 1.0, 0.0
        ).astype(BF16)
        picked = jnp.dot(table_ref[...], hot, preferred_element_type=F32)
        near = picked[0:padded] + picked[padded:2 * padded] + picked[2 * padded:3 * padded]
        far = picked[3 * padded:4 * padded] + picked[4 * padded:5 * padded] + picked[5 * padded:6 * padded]
        tail = picked[6 * padded:6 * padded + 16]
        cycles = lax.broadcasted_iota(jnp.int32, (padded, CHUNK), 0)
        here = cycles == cycle0
        below = cycles == cycle0 + 1

        def take(mask, field):
            return jnp.sum(jnp.where(mask, field, 0.0), axis=0, keepdims=True)

        radius_of = ((take(here, near), take(here, far)), (take(below, near), take(below, far)))
        cycle_hot = jnp.where(here, 1.0, 0.0).astype(BF16)
        turn = jnp.dot(polar_rows_ref[...], cycle_hot, preferred_element_type=F32)

        def join(rows, start):
            return rows[start:start + 1] + rows[start + 1:start + 2] + rows[start + 2:start + 3]

        sin_t = (join(turn, 0), join(turn, 6))
        cos_t = (join(turn, 3), join(turn, 9))
        cos_f = (join(tail, 0), join(tail, 6))
        sin_f = (join(tail, 3), join(tail, 9))
        points = []
        for k in range(3):
            down = cycle_k[k] != cycle0
            side = azim_k[k] != azim0
            radius_k = jnp.where(
                down,
                jnp.where(side, radius_of[1][1], radius_of[1][0]),
                jnp.where(side, radius_of[0][1], radius_of[0][0]),
            )
            ring = radius_k * jnp.where(down, sin_t[1], sin_t[0])
            points.append((
                ring * jnp.where(side, cos_f[1], cos_f[0]),
                ring * jnp.where(side, sin_f[1], sin_f[0]),
                radius_k * jnp.where(down, cos_t[1], cos_t[0]),
            ))
        return points

    def center_of(points):
        return [(points[0][axis] + points[1][axis] + points[2][axis]) / 3.0 for axis in range(3)]

    def target_chunk(turn, carry):
        first = pl.multiple_of((2 * turn + side_of_pair) * src_dev, src_dev)
        center = center_of(corners_of(conn_ref[:, pl.ds(first, CHUNK)]))
        place = pl.ds(pl.multiple_of(turn * CHUNK, CHUNK), CHUNK)
        for axis in range(3):
            target_c_ref[axis:axis + 1, place] = center[axis]
            high, mid, low = [part.astype(F32) for part in split3(center[axis])]
            for index, part in enumerate((high, high, high, mid, mid, low)):
                rows_ref[6 * axis + index:6 * axis + index + 1, :] = part
        rows_ref[18:21, :] = jnp.ones((3, CHUNK), F32)
        target_k_ref[:, place] = rows_ref[0:KDIM, :].astype(BF16)
        return carry

    def source_chunk(turn, carry):
        first = pl.multiple_of((me - side_of_pair) * src_dev + turn * CHUNK, CHUNK)
        points = corners_of(conn_ref[:, pl.ds(first, CHUNK)])
        center = center_of(points)
        one = [points[1][axis] - points[0][axis] for axis in range(3)]
        two = [points[2][axis] - points[0][axis] for axis in range(3)]
        factor = 0.5 / (4.0 * math.pi)
        area = [
            factor * (one[1] * two[2] - one[2] * two[1]),
            factor * (one[2] * two[0] - one[0] * two[2]),
            factor * (one[0] * two[1] - one[1] * two[0]),
        ]
        for axis in range(3):
            high, mid, low = [part.astype(F32) for part in split3(area[axis])]
            for index, part in enumerate((high, mid, low, high, mid, high)):
                rows_ref[6 * axis + index:6 * axis + index + 1, :] = part
        base = -(center[0] * area[0] + center[1] * area[1] + center[2] * area[2])
        for index, part in enumerate(split3(base)):
            rows_ref[18 + index:19 + index, :] = part.astype(F32)
        for axis in range(3):
            rows_ref[KDIM + axis:KDIM + axis + 1, :] = center[axis]
        turned = rows_ref[...].T
        place = pl.ds(pl.multiple_of(turn * CHUNK, CHUNK), CHUNK)
        source_k_ref[place, :] = turned[:, 0:KDIM].astype(BF16)
        for axis in range(3):
            source_b_ref[axis, place, :] = jnp.broadcast_to(
                turned[:, KDIM + axis:KDIM + axis + 1], (CHUNK, 128)
            )
        return carry

    lax.fori_loop(0, 2 * src_dev // CHUNK, source_chunk, 0, unroll=8)
    lax.fori_loop(0, row_total // 2, target_chunk, 0, unroll=8)


def kernel(
    padded, src_dev, row_total,
    sample_ref, conn_hbm, density_hbm, lattice_hbm, mode_hbm, pol_hbm, azi_hbm, azim_rows_hbm,
    polar_rows_hbm,
    out_ref,
    conn_ref, density_ref, lattice_ref, mode_ref, pol_ref, azi_ref, azim_rows_ref, polar_rows_ref,
    target_k_ref, target_c_ref, source_k_ref, source_b_ref, table_ref, rows_ref,
    send_buf, recv_buf, load_sem, share_sem, send_sem, recv_sem,
):
    me = lax.axis_index("row")
    side = lax.rem(me, 2)
    sibling = me + 1 - 2 * side
    owners = row_total // 2
    own_half = pl.ds(pl.multiple_of(side * src_dev, src_dev), src_dev)
    loads = [
        pltpu.make_async_copy(source, place, load_sem.at[index])
        for index, (source, place) in enumerate((
            (conn_hbm, conn_ref), (density_hbm, density_ref.at[:, own_half]), (lattice_hbm, lattice_ref),
            (mode_hbm, mode_ref), (pol_hbm, pol_ref), (azi_hbm, azi_ref),
            (azim_rows_hbm, azim_rows_ref), (polar_rows_hbm, polar_rows_ref),
        ))
    ]
    for index in (3, 2, 5, 4, 6, 7, 0, 1):
        loads[index].start()
    peers = owners - 1

    def owner_of(turn):
        return 2 * lax.rem(me // 2 + 1 + turn, owners) + side

    barrier = pltpu.get_barrier_semaphore()
    pl.semaphore_signal(
        barrier, inc=1, device_id={"row": sibling}, device_id_type=pl.DeviceIdType.MESH
    )

    def greet(turn, carry):
        pl.semaphore_signal(
            barrier, inc=1, device_id={"row": owner_of(turn)}, device_id_type=pl.DeviceIdType.MESH
        )
        return carry

    lax.fori_loop(0, peers, greet, 0)
    share = pltpu.make_async_remote_copy(
        src_ref=density_ref.at[:, own_half],
        dst_ref=density_ref.at[:, own_half],
        send_sem=share_sem.at[0],
        recv_sem=share_sem.at[1],
        device_id={"row": sibling},
        device_id_type=pl.DeviceIdType.MESH,
    )

    def begin():
        loads[0].wait()
        loads[1].wait()
        pl.semaphore_wait(barrier, peers + 1)
        share.start()

    for load in loads[2:]:
        load.wait()
    geometry(
        padded, src_dev, row_total, begin,
        sample_ref, lattice_ref, mode_ref, conn_ref, pol_ref, azi_ref, azim_rows_ref,
        polar_rows_ref, target_k_ref, target_c_ref, source_k_ref, source_b_ref,
        table_ref, rows_ref,
    )
    share.wait()

    def block(place_index, own):
        place = pl.ds(pl.multiple_of(place_index * BAND_DEV, BAND_DEV), BAND_DEV)
        target_k = target_k_ref[:, place]
        target = [target_c_ref[axis:axis + 1, place] for axis in range(3)]
        def numerator(first):
            return jnp.dot(
                source_k_ref[first:first + SRC_TILE, :], target_k, preferred_element_type=F32
            )

        def weigh(first, tile):
            return jnp.dot(
                density_ref[:, first:first + SRC_TILE], tile, preferred_element_type=F32
            )

        total = jnp.zeros((density_ref.shape[0], BAND_DEV), F32)
        top = numerator(0)
        before = None
        for first in range(0, 2 * src_dev, SRC_TILE):
            following = numerator(first + SRC_TILE) if first + SRC_TILE < 2 * src_dev else None
            part = slice(first, first + SRC_TILE)
            dist = None
            for axis in range(3):
                wide = source_b_ref[axis, part, :]
                diff = target[axis] - jnp.concatenate([wide] * (BAND_DEV // 128), axis=1)
                dist = diff * diff if dist is None else dist + diff * diff
            if own and first % src_dev < BAND_DEV:
                same = (
                    lax.broadcasted_iota(jnp.int32, dist.shape, 0) + first
                    == lax.broadcasted_iota(jnp.int32, dist.shape, 1) + side * src_dev
                )
                inverse = lax.rsqrt(jnp.where(same, 1.0, dist))
                tile = jnp.where(same, 0.0, top * inverse * (inverse * inverse))
            else:
                inverse = lax.rsqrt(dist)
                tile = top * inverse * (inverse * inverse)
            tile = tile.astype(BF16)
            if before is not None:
                total += weigh(first - SRC_TILE, before)
            before = tile
            top = following
        return total + weigh(2 * src_dev - SRC_TILE, before)

    def copy(turn):
        return pltpu.make_async_remote_copy(
            src_ref=send_buf.at[turn],
            dst_ref=recv_buf.at[turn],
            send_sem=send_sem.at[turn],
            recv_sem=recv_sem.at[turn],
            device_id={"row": owner_of(turn)},
            device_id_type=pl.DeviceIdType.MESH,
        )

    def step(turn, carry):
        send_buf[turn] = block(lax.rem(me // 2 + 1 + turn, owners), False).astype(BF16)
        copy(turn).start()
        return carry

    lax.fori_loop(0, peers, step, 0)
    local = density_ref[:, pl.ds(pl.multiple_of(side * src_dev, src_dev), BAND_DEV)]
    out_ref[...] = block(me // 2, True) + 0.5 * local.astype(F32)

    def collect(turn, carry):
        copy(turn).wait_recv()
        out_ref[...] += recv_buf[turn].astype(F32)
        return carry

    lax.fori_loop(0, peers, collect, 0)

    def finish(turn, carry):
        copy(turn).wait_send()
        return carry

    lax.fori_loop(0, peers, finish, 0)


def per_device(sample_index, lattice_vector, mode_table, connectivity, density):
    columns, src_dev = density.shape
    row_total = lax.axis_size("row")
    panel_total = src_dev * row_total
    cycle_count = panel_total // (2 * NPH) + 1
    padded = round_up(cycle_count, 16)
    band = BAND_DEV * row_total
    pol, azi, azim_rows, polar_rows = [jnp.asarray(t) for t in tables(cycle_count, padded)]
    vmem = pl.BlockSpec(memory_space=pltpu.VMEM)
    smem = pl.BlockSpec(memory_space=pltpu.SMEM)
    hbm = pl.BlockSpec(memory_space=pltpu.HBM)
    loaded = [
        connectivity, density, lattice_vector.reshape(1, -1), mode_table,
        pol, azi, azim_rows, polar_rows,
    ]
    sums = pl.pallas_call(
        functools.partial(kernel, padded, src_dev, row_total),
        out_shape=jax.ShapeDtypeStruct((columns, BAND_DEV), F32),
        in_specs=[smem] + [hbm] * len(loaded),
        out_specs=vmem,
        scratch_shapes=[
            pltpu.VMEM(connectivity.shape, jnp.int32),
            pltpu.VMEM((columns, 2 * src_dev), BF16),
        ] + [pltpu.VMEM(array.shape, array.dtype) for array in loaded[2:]] + [
            pltpu.VMEM((KDIM, band // 2), BF16),
            pltpu.VMEM((3, band // 2), F32),
            pltpu.VMEM((2 * src_dev, KDIM), BF16),
            pltpu.VMEM((3, 2 * src_dev, 128), F32),
            pltpu.VMEM((6 * padded + 16, NPH), BF16),
            pltpu.VMEM((KDIM + 8, CHUNK), F32),
            pltpu.VMEM((row_total // 2 - 1, columns, BAND_DEV), BF16),
            pltpu.VMEM((row_total // 2 - 1, columns, BAND_DEV), BF16),
            pltpu.SemaphoreType.DMA((len(loaded),)),
            pltpu.SemaphoreType.DMA((2,)),
            pltpu.SemaphoreType.DMA((row_total // 2 - 1,)),
            pltpu.SemaphoreType.DMA((row_total // 2 - 1,)),
        ],
        compiler_params=pltpu.CompilerParams(
            collective_id=0, has_side_effects=True, vmem_limit_bytes=63 << 20
        ),
        name="potential",
    )(sample_index, *loaded)
    return sums.T


def solution(mesh):
    placed = (P("sample"), P(), P(), P(), P(None, "row"))
    return jax.shard_map(
        per_device,
        mesh=mesh,
        in_specs=placed,
        out_specs=P(("sample", "row"), None),
        check_vma=False,
    )
```
